32 devices in a mesh: row: 2 (over y), col: 4 (over z), rep: 4 (over x, core).
Axes of the slice: x: 2, y: 2, z: 4, core: 2. Of those that a mesh axis runs over, the one named last changes fastest.
Arguments:
- amplitudes: float32 [18432, 18432], P('row', ('col', 'rep')), may hold values from -0.046875 to 0.046875
- cycle_ints: float32 [18432, 288], P(('col', 'rep'), 'row'), may hold values from -6 to 6
Outputs:
- cycle_term: float32 [18432, 288], P(('row', 'rep'), 'col')
The draws below stay inside these ranges and needn't reach their ends.
All inputs are finite; a program needn't handle non-finite values.
Results may differ from the reference program's by a relative error of at most 0.0002.
Values sent between devices are 32-bit elements; how exact they have to be, the bound alone decides.
No kernel may reach another device: no remote copies, remote signals or barrier semaphores. Data moves between devices by JAX's collectives and lax.ppermute only.
A program may use at most 128 MiB of HBM per device.

```python
import jax
import jax.numpy as jnp
from jax import lax

PAIRS = 18432
WINDOW = 288


def raised(drawn, stream_key, source, target, shards_of, factor):
    def block_of(position):
        return (jnp.arange(drawn.shape[position]) // (drawn.shape[position] // shards_of)).reshape((-1,) + (1,) * (drawn.ndim - 1 - position))

    near = jax.random.permutation(stream_key, shards_of)[block_of(target)]
    far = (block_of(target) + shards_of // 2) % shards_of
    return jnp.where((block_of(source) == near) | (block_of(source) == far), factor * drawn, drawn)


def level_of(stream_key, dims, pieces, low, top_value):
    def one(axis_at, shards_of):
        draws = jax.random.uniform(jax.random.fold_in(jax.random.fold_in(stream_key, 6), axis_at), (shards_of,), jnp.float32, low / len(pieces), top_value / len(pieces))
        return jnp.repeat(jnp.exp(draws), dims[axis_at] // shards_of).reshape((-1,) + (1,) * (len(dims) - axis_at - 1))

    gain = one(*pieces[0])
    for cut in pieces[1:]:
        gain = gain * one(*cut)
    return gain


def centred(own_key, shape, scale, bound, pieces=(), kind=jnp.bfloat16):
    array = scale * jax.random.normal(own_key, shape, jnp.float32)
    if pieces:
        array = array * level_of(own_key, shape, pieces, -0.22, 0.18)
    return jnp.clip(array, -bound, bound).astype(kind)


def gaussian_with(own_key, dims, width, limit, pieces, heavy, held_as=jnp.bfloat16):
    drawn = width * jax.random.normal(own_key, dims, jnp.float32)
    if pieces:
        drawn = drawn * level_of(own_key, dims, pieces, -0.22, 0.18)
    return jnp.clip(raised(drawn, jax.random.fold_in(own_key, 3), *heavy), -limit, limit).astype(held_as)


def setup_inputs(seed: int = 0) -> dict:
    splits = jax.random.split(jax.random.key(seed), 3)
    amplitudes = centred(splits[0], (PAIRS, PAIRS), PAIRS ** -0.5, 0.046875, ((0, 2), (1, 16)), jnp.float32)
    cycle_ints = gaussian_with(splits[1], (PAIRS, WINDOW), 1.0, 6.0, ((0, 16), (1, 2)), (0, 1, 16, 2.0), jnp.float32)
    return dict(amplitudes=amplitudes, cycle_ints=cycle_ints)


def reference(amplitudes, cycle_ints):
    return jnp.dot(amplitudes, cycle_ints, precision=lax.Precision.HIGHEST, preferred_element_type=jnp.float32)
```

```python
import functools

import jax
import jax.numpy as jnp
from jax import lax
from jax.experimental import pallas as pl
from jax.experimental.pallas import tpu as pltpu
from jax.sharding import PartitionSpec as P

LANES = 128
PIECES = (2, 4, 4, 4, 3, 1)
CONTRACT_LAST = (((1,), (1,)), ((), ()))


def halves(x):
    high = x.astype(jnp.bfloat16)
    return high, (x - high.astype(jnp.float32)).astype(jnp.bfloat16)


def split_kernel(swap_ref, own_ref, other_ref, high_ref, low_ref):
    high_ref[0], low_ref[0] = halves(jnp.where(pl.program_id(0) == 0, own_ref[...], other_ref[...]))


def split_ints(own, other, row):
    width, depth = own.shape
    whole = pl.BlockSpec((width, depth), lambda i, swap: (0, 0))
    target = pl.BlockSpec((1, width, depth), lambda i, swap: (i ^ swap[0], 0, 0))
    high, low = pl.pallas_call(
        split_kernel,
        out_shape=[jax.ShapeDtypeStruct((2, width, depth), jnp.bfloat16)] * 2,
        grid_spec=pltpu.PrefetchScalarGridSpec(
            num_scalar_prefetch=1, grid=(2,), in_specs=[whole, whole], out_specs=[target, target]
        ),
        name="split_ints",
    )(row.reshape(1), own, other)
    return high.reshape(2 * width, depth), low.reshape(2 * width, depth)


def product(rows, high_ref, low_ref):
    high, low = halves(rows)
    dot = functools.partial(
        lax.dot_general, dimension_numbers=CONTRACT_LAST, preferred_element_type=jnp.float32
    )
    return dot(high_ref[...], high) + (dot(low_ref[...], high) + dot(high_ref[...], low))


def tile_of(width):
    for tile in (4, 3, 2, 1):
        if width % tile == 0:
            return tile


def products(amplitudes, high, low, blocks, start, width, addend=None, addend_blocks=None):
    n_blocks = blocks.shape[0]
    n_cols, depth = high.shape
    tile = tile_of(width)
    tiles = width // tile
    block_rows = amplitudes.shape[0] // 4 // LANES
    row_at = (blocks[:, None] * block_rows + start + tile * jnp.arange(tiles)[None]).reshape(-1)
    size = tile * LANES
    scalars = [row_at.astype(jnp.int32)]
    resident = pl.BlockSpec((n_cols, depth), lambda i, *s: (0, 0))
    in_specs = [
        pl.BlockSpec((pl.Element(size), pl.Element(depth)), lambda i, at, *s: (at[i] * LANES, 0)),
        resident,
        resident,
    ]
    args = [amplitudes, high, low]
    if addend is not None:
        scalars.append(addend_blocks.astype(jnp.int32))
        in_specs.append(
            pl.BlockSpec((1, n_cols, size), lambda i, at, which: (which[i // tiles], 0, i % tiles))
        )
        args.append(addend)

    def kernel(*refs):
        refs = refs[len(scalars):]
        result = product(refs[0][...], refs[1], refs[2])
        if addend is not None:
            result = result + refs[3][0]
        refs[-1][0] = result

    rows = n_blocks * width * LANES
    return pl.pallas_call(
        kernel,
        out_shape=jax.ShapeDtypeStruct((n_blocks, n_cols, width * LANES), jnp.float32),
        grid_spec=pltpu.PrefetchScalarGridSpec(
            num_scalar_prefetch=len(scalars),
            grid=(n_blocks * tiles,),
            in_specs=in_specs,
            out_specs=pl.BlockSpec((1, n_cols, size), lambda i, *s: (i // tiles, 0, i % tiles)),
        ),
        compiler_params=pltpu.CompilerParams(vmem_limit_bytes=32 << 20),
        cost_estimate=pl.CostEstimate(
            flops=6 * rows * n_cols * depth, bytes_accessed=4 * rows * depth, transcendentals=0
        ),
        name="products",
    )(*scalars, *args)


def pipelined(amplitudes, cycle_ints):
    row, col, rep = (lax.axis_index(axis) for axis in ("row", "col", "rep"))
    chip, core = rep // 2, rep % 2
    own = cycle_ints.T
    other = lax.ppermute(own, "row", [(0, 1), (1, 0)])
    high, low = split_ints(own, other, row)
    n_cols = high.shape[0]
    width = n_cols // 4
    swap_core = [(i, i ^ 1) for i in range(4)]
    swap_chip = [(i, i ^ 2) for i in range(4)]
    ring = [(i, (i + 1) % 4) for i in range(4)]
    scale = amplitudes.shape[0] // 4 // LANES // sum(PIECES)

    sibling_blocks = jnp.stack([1 - core, 3 - core])
    far = (2 * (1 - chip) + core).reshape(1)
    near = (2 * chip + core).reshape(1)

    outs = []
    start = 0
    for piece in PIECES:
        piece = piece * scale
        lanes = piece * LANES
        for_sibling = products(amplitudes, high, low, sibling_blocks, start, piece)
        from_sibling = lax.ppermute(for_sibling, "rep", swap_core)
        for_far = products(
            amplitudes, high, low, far, start, piece, from_sibling, (1 - chip).reshape(1)
        )
        from_far = lax.ppermute(for_far, "rep", swap_chip).reshape(4, width, lanes)
        mine = products(
            amplitudes, high, low, near, start, piece, from_sibling, chip.reshape(1)
        ).reshape(4, width, lanes)

        def part(step):
            at = (col - step) % 4
            return mine[at] + from_far[at]

        carried = part(1)
        for step in (2, 3, 4):
            carried = lax.ppermute(carried, "col", ring) + part(step)
        outs.append(carried)
        start += piece
    return jnp.concatenate(outs, 1).T


def passed_along(x, axis, by):
    devices = lax.axis_size(axis)
    return lax.ppermute(x, axis, [(i, (i + by) % devices) for i in range(devices)])


def general(amplitudes, cycle_ints):
    n_col = lax.axis_size("col")
    full_ints = lax.all_gather(cycle_ints, "row", axis=1, tiled=True)
    width = full_ints.shape[1] // n_col
    here = lax.axis_index("col")
    n_rows = amplitudes.shape[0]

    def advance(step, partial_sum):
        block = (here - step) % n_col
        columns = lax.dynamic_slice_in_dim(full_ints, block * width, width, 1)
        partial_sum = partial_sum + jnp.dot(
            amplitudes, columns, precision=lax.Precision.HIGHEST, preferred_element_type=jnp.float32
        )
        return passed_along(partial_sum, "col", 1)

    totals = lax.fori_loop(0, n_col, advance, jnp.zeros((n_rows, width), jnp.float32))
    return lax.psum_scatter(totals, "rep", scatter_dimension=0, tiled=True)


def per_device(amplitudes, cycle_ints):
    sizes = tuple(lax.axis_size(axis) for axis in ("row", "col", "rep"))
    rows, depth = amplitudes.shape
    fits = rows % (4 * LANES * sum(PIECES)) == 0 and depth % LANES == 0
    if sizes == (2, 4, 4) and fits and cycle_ints.shape[1] % 16 == 0:
        return pipelined(amplitudes, cycle_ints)
    return general(amplitudes, cycle_ints)


def solution(mesh):
    return jax.shard_map(
        per_device,
        mesh=mesh,
        in_specs=(P("row", ("col", "rep")), P(("col", "rep"), "row")),
        out_specs=P(("row", "rep"), "col"),
        check_vma=False,
    )
```

```python
import functools
import math
import re

import jax
import jax.numpy as jnp
from jax import lax
from jax.experimental import pallas as pl
from jax.experimental.pallas import tpu as pltpu
from jax.sharding import PartitionSpec as P


LANES = 128
SLOTS = 3
PAIR = 2
PIECES = (4, 4, 4, 2, 2, 2)
ORDER = (
    "S0a", "T0a", "S0b", "S1ab", "T0b", "T1S2ab", "Z0a", "Z0b", "T2S3ab", "F0", "T3S4ab", "Z1ab", "T4S5ab",
    "Z2ab", "F1", "T5ab", "Z3ab", "F2", "Z4ab", "F3", "Z5ab", "F4", "F5",
)
EVENT = re.compile(r"(?:T(\d))?(?:S(\d))?(?:([ZF])(\d))?([ab]*)$")
CONTRACT_LAST = (((1,), (1,)), ((), ()))
VMEM = pl.BlockSpec(memory_space=pltpu.VMEM)


def halves(x):
    high = x.astype(jnp.bfloat16)
    return high, (x - high.astype(jnp.float32)).astype(jnp.bfloat16)


def products(place, amplitudes, ints, close, beside):
    depth = amplitudes.shape[1]
    n_cols = sum(part.shape[0] for part in ints)
    block_rows = amplitudes.shape[0] // 4 // LANES
    size = PAIR * LANES
    n_close = close[1] // PAIR if close else 0
    n_beside = beside[1] // PAIR if beside else 0
    tiles = n_close + n_beside
    slots = min(SLOTS, tiles)
    args = [amplitudes, *ints]
    out_shape = []
    if close:
        args.append(close[2])
        out_shape += [jax.ShapeDtypeStruct((1, n_cols, close[1] * LANES), jnp.float32)] * 2
    if beside:
        out_shape.append(jax.ShapeDtypeStruct((2, n_cols, beside[1] * LANES), jnp.float32))

    def kernel(place_ref, rows_ref, *refs):
        *refs, high_ref, low_ref, held, arrived = refs
        ints_refs, rest = refs[: len(ints)], refs[len(ints):]

        def fetch(tile, half):
            chip, core = place_ref[2] >> 1, place_ref[2] & 1
            if tile < n_close:
                block = 2 * (chip if half else 1 - chip) + core
                at = close[0] + tile * PAIR
            else:
                block = 2 * half + 1 - core
                at = beside[0] + (tile - n_close) * PAIR
            first = pl.multiple_of((block * block_rows + at) * LANES, LANES)
            slot = tile % slots
            return pltpu.make_async_copy(
                rows_ref.at[pl.ds(first, size), :],
                held.at[slot, pl.ds(half * size, size), :],
                arrived.at[slot, half],
            )

        for tile in range(slots):
            for half in range(2):
                fetch(tile, half).start()
        at = 0
        for ref in ints_refs:
            to = pl.ds(at, ref.shape[0])
            high_ref[to, :], low_ref[to, :] = halves(ref[...])
            at += ref.shape[0]
        dot = functools.partial(
            lax.dot_general, dimension_numbers=CONTRACT_LAST, preferred_element_type=jnp.float32
        )
        for tile in range(tiles):
            for half in range(2):
                fetch(tile, half).wait()
            a_high, a_low = halves(held[tile % slots])
            result = dot(high_ref[...], a_high) + (
                dot(low_ref[...], a_high) + dot(high_ref[...], a_low)
            )
            if tile < n_close:
                came_ref, far_ref, near_ref = rest[:3]
                chip_here = place_ref[2] >> 1
                lanes = pl.ds(tile * size, size)
                far_ref[0, :, lanes] = result[:, :size] + came_ref[1 - chip_here, :, lanes]
                near_ref[0, :, lanes] = result[:, size:] + came_ref[chip_here, :, lanes]
            else:
                lanes = pl.ds((tile - n_close) * size, size)
                rest[-1][0, :, lanes] = result[:, :size]
                rest[-1][1, :, lanes] = result[:, size:]
            if tile + slots < tiles:
                for half in range(2):
                    fetch(tile + slots, half).start()

    rows = 2 * tiles * size
    return pl.pallas_call(
        kernel,
        out_shape=out_shape,
        grid_spec=pltpu.PrefetchScalarGridSpec(
            num_scalar_prefetch=1,
            grid=(),
            in_specs=[pl.BlockSpec(memory_space=pl.ANY)] + [VMEM] * (len(args) - 1),
            out_specs=[VMEM] * len(out_shape),
            scratch_shapes=[pltpu.VMEM((n_cols, depth), jnp.bfloat16)] * 2
            + [
                pltpu.VMEM((slots, 2 * size, depth), jnp.float32),
                pltpu.SemaphoreType.DMA((slots, 2)),
            ],
        ),
        compiler_params=pltpu.CompilerParams(vmem_limit_bytes=17 << 20),
        cost_estimate=pl.CostEstimate(
            flops=6 * rows * n_cols * depth, bytes_accessed=4 * rows * depth, transcendentals=0
        ),
        name="products",
    )(place, *args)


def small(kernel, shapes, place, args):
    size = 4 * sum(math.prod(shape) for shape in shapes) + sum(4 * x.size for x in args)
    return pl.pallas_call(
        kernel,
        out_shape=[jax.ShapeDtypeStruct(shape, jnp.float32) for shape in shapes],
        grid_spec=pltpu.PrefetchScalarGridSpec(
            num_scalar_prefetch=1,
            grid=(),
            in_specs=[VMEM] * len(args),
            out_specs=[VMEM] * len(shapes),
        ),
        compiler_params=pltpu.CompilerParams(vmem_limit_bytes=8 << 20),
        cost_estimate=pl.CostEstimate(flops=size, bytes_accessed=size, transcendentals=0),
        name="sums",
    )(place, *args)


def z_kernel(place_ref, near_ref, far_ref, sent_ref, keeps_ref):
    bit = place_ref[1] & 1
    for part in range(near_ref.shape[0]):
        sent_ref[part] = near_ref[part, 1 - bit] + far_ref[part, 1 - bit]
        keeps_ref[part] = near_ref[part, bit] + far_ref[part, bit]


def f_kernel(place_ref, *refs):
    *sums, sent_ref, stays_ref = refs
    half = (place_ref[1] >> 1) ^ place_ref[0]
    if len(sums) == 2:
        keeps_ref, came_ref = sums
        sent_ref[...] = keeps_ref[1 - half] + came_ref[1 - half]
        stays_ref[...] = keeps_ref[half] + came_ref[half]
        return
    own = sums[0][0] + sums[1][0]
    other = sums[2][0] + sums[3][0]
    sent_ref[...] = jnp.where(half == 0, other, own)
    stays_ref[...] = jnp.where(half == 0, own, other)


def end_kernel(_, *refs):
    at = 0
    for stays_ref, came_ref in zip(refs[:-1:2], refs[1:-1:2]):
        to = pl.ds(at, stays_ref.shape[1])
        refs[-1][:, to] = stays_ref[...] + came_ref[...]
        at += stays_ref.shape[1]


def pipelined(amplitudes, cycle_ints):
    place = jnp.stack([lax.axis_index(axis) for axis in ("row", "col", "rep")]).astype(jnp.int32)
    flip = {bit: [(i, i ^ bit) for i in range(4)] for bit in (1, 2)}

    own = cycle_ints.T
    other = lax.ppermute(own, "row", [(0, 1), (1, 0)])
    sets = {"a": (own,), "b": (other,), "ab": (own, other)}
    width = own.shape[0] // 2
    scale = amplitudes.shape[0] // 4 // LANES // sum(PIECES)
    starts = [sum(PIECES[:i]) * scale for i in range(len(PIECES))]
    units = [piece * scale for piece in PIECES]

    got, far, near, kept, outs = {}, {}, {}, {}, {}
    for event in ORDER:
        close, beside, kind, piece, part = EVENT.match(event).groups()
        shape = (len(part), 2, width, -1)
        if close or beside:
            c, b = close and int(close), beside and int(beside)
            made = products(
                place,
                amplitudes,
                sets[part],
                (starts[c], units[c], got[c, part]) if close else None,
                (starts[b], units[b]) if beside else None,
            )
            if close:
                far[c, part] = lax.ppermute(made[0], "rep", flip[2]).reshape(shape)
                near[c, part] = made[1].reshape(shape)
            if beside:
                got[b, part] = lax.ppermute(made[-1], "rep", flip[1])
            continue
        piece = int(piece)
        key = (piece, part)
        if kind == "Z":
            sent, keeps = small(z_kernel, [(len(part), width, units[piece] * LANES)] * 2, place, [near[key], far[key]])
            kept[key] = keeps, lax.ppermute(sent, "col", flip[1])
        elif kind == "F":
            sums = [x for k in kept if k[0] == piece for x in kept[k]]
            sent, stays = small(f_kernel, [(width, units[piece] * LANES)] * 2, place, sums)
            outs[piece] = stays, lax.ppermute(sent, "col", flip[2])
    pairs = [x for p in range(len(PIECES)) for x in outs[p]]
    return small(end_kernel, [(width, sum(units) * LANES)], place, pairs)[0].T


def passed_along(x, axis, by):
    devices = lax.axis_size(axis)
    return lax.ppermute(x, axis, [(i, (i + by) % devices) for i in range(devices)])


def general(amplitudes, cycle_ints):
    n_col = lax.axis_size("col")
    full_ints = lax.all_gather(cycle_ints, "row", axis=1, tiled=True)
    width = full_ints.shape[1] // n_col
    here = lax.axis_index("col")
    n_rows = amplitudes.shape[0]

    def advance(step, partial_sum):
        block = (here - step) % n_col
        columns = lax.dynamic_slice_in_dim(full_ints, block * width, width, 1)
        partial_sum = partial_sum + jnp.dot(
            amplitudes, columns, precision=lax.Precision.HIGHEST, preferred_element_type=jnp.float32
        )
        return passed_along(partial_sum, "col", 1)

    totals = lax.fori_loop(0, n_col, advance, jnp.zeros((n_rows, width), jnp.float32))
    return lax.psum_scatter(totals, "rep", scatter_dimension=0, tiled=True)


def tall_enough(amplitudes, cycle_ints):
    rows, depth = amplitudes.shape
    return rows % (4 * LANES * sum(PIECES)) == 0 and depth % LANES == 0 and cycle_ints.shape[1] % 16 == 0


def solution(mesh):
    sizes = tuple(mesh.shape[axis] for axis in ("row", "col", "rep"))

    def per_device(amplitudes, cycle_ints):
        if sizes == (2, 4, 4) and tall_enough(amplitudes, cycle_ints):
            return pipelined(amplitudes, cycle_ints)
        return general(amplitudes, cycle_ints)

    return jax.shard_map(
        per_device,
        mesh=mesh,
        in_specs=(P("row", ("col", "rep")), P(("col", "rep"), "row")),
        out_specs=P(("row", "rep"), "col"),
        check_vma=False,
    )
```
